32 devices in a mesh: grp: 4 (over y, x), tok: 8 (over z, core).
Axes of the slice: x: 2, y: 2, z: 4, core: 2. Of those that a mesh axis runs over, the one named last changes fastest.
Arguments:
- queries: bfloat16 [4096, 768], P(('grp', 'tok')), may hold values from -6 to 6
- key_tokens: float32 [4096, 768], P(('grp', 'tok')), may hold values from -6 to 6
- values: float32 [4096, 768], P(('grp', 'tok')), may hold values from -6 to 6
- out_grad: bfloat16 [4096, 768], P(('grp', 'tok')), may hold values from -6 to 6
- w_gate: float32 [768, 768], replicated, may hold values from -0.21875 to 0.21875
- w_up: float32 [768, 768], replicated, may hold values from -0.21875 to 0.21875
- w_down: float32 [768, 768], replicated, may hold values from -0.21875 to 0.21875
Outputs:
- d_queries: bfloat16 [4096, 768], P(('grp', 'tok'))
- d_keys: float32 [4096, 768], P(('grp', 'tok'))
- d_values: float32 [4096, 768], P(('grp', 'tok'))
- d_gate: float32 [768, 768], P('tok')
- d_up: float32 [768, 768], P('tok')
- d_down: float32 [768, 768], P('tok')
The draws below stay inside these ranges and needn't reach their ends.
All inputs are finite; a program needn't handle non-finite values.
Results may differ from the reference program's by a relative error of at most 0.012.
Values may be sent and summed in bfloat16 or wider, within the bound.
A program may use at most 128 MiB of HBM per device.

```python
import jax
import jax.numpy as jnp
from jax import lax

D = 768
TOK_DEV = 128
TOKENS = 4096


def block_scale(key, dims, pieces, low, high):
    def one(axis_at, shards_of):
        steps = jax.random.uniform(jax.random.fold_in(jax.random.fold_in(key, 6), axis_at), (shards_of,), jnp.float32, low / len(pieces), high / len(pieces))
        return jnp.repeat(jnp.exp(steps), dims[axis_at] // shards_of).reshape((-1,) + (1,) * (len(dims) - axis_at - 1))

    gain = one(*pieces[0])
    for cut in pieces[1:]:
        gain = gain * one(*cut)
    return gain


def centred(key, dims, width, limit, shards=(), kind=jnp.bfloat16):
    values = jax.random.normal(key, dims, jnp.float32) * width
    if len(shards) > 0:
        values = block_scale(key, dims, shards, -0.22, 0.18) * values
    return jnp.clip(values, min=-limit, max=limit).astype(kind)


def setup_inputs(seed: int = 0) -> dict:
    keys = jax.random.split(jax.random.key(seed), 8)
    return {
        "queries": centred(keys[0], (TOKENS, D), 1.0, 6.0, ((0, 32),)),
        "key_tokens": centred(keys[1], (TOKENS, D), 1.0, 6.0, ((0, 32),), jnp.float32),
        "values": centred(keys[2], (TOKENS, D), 1.0, 6.0, ((0, 32),), jnp.float32),
        "out_grad": centred(keys[3], (TOKENS, D), 1.0, 6.0, ((0, 32),)),
        "w_gate": centred(keys[4], (D, D), D ** -0.5, 0.21875, (), jnp.float32),
        "w_up": centred(keys[5], (D, D), D ** -0.5, 0.21875, (), jnp.float32),
        "w_down": centred(keys[6], (D, D), D ** -0.5, 0.21875, (), jnp.float32),
    }


STEP_SIZE = 0.02
EPSILON = 1e-06
HIGH = lax.Precision.HIGHEST

def matmul(left, right):
    return jnp.dot(left, right, precision=HIGH, preferred_element_type=jnp.float32)

def key_grad(w_gate, w_up, w_down, key_rows, value_rows):
    hidden_gate = matmul(key_rows, w_gate)
    hidden_up = matmul(key_rows, w_up)
    sig = jax.nn.sigmoid(hidden_gate)
    active = hidden_gate * sig * hidden_up
    error = matmul(active, w_down) - value_rows
    d_active = matmul(error, w_down.T)
    d_hup = d_active * hidden_gate * sig
    d_hgate = d_active * hidden_up * sig * (1.0 + hidden_gate * (1.0 - sig))
    return (matmul(key_rows.T, d_hgate), matmul(key_rows.T, d_hup), matmul(active.T, error))

def query_grad(fast_weights, query_rows, grad_rows):
    fast_gate, fast_up, fast_down = fast_weights
    hidden_gate = jnp.dot(query_rows, fast_gate, preferred_element_type=jnp.float32)
    hidden_up = jnp.dot(query_rows, fast_up, preferred_element_type=jnp.float32)
    sig = jax.nn.sigmoid(hidden_gate)
    active = (hidden_gate * sig * hidden_up).astype(jnp.bfloat16)
    d_active = jnp.dot(grad_rows, fast_down.T, preferred_element_type=jnp.float32)
    d_hup = (d_active * hidden_gate * sig).astype(jnp.bfloat16)
    d_hgate = (d_active * hidden_up * sig * (1.0 + hidden_gate * (1.0 - sig))).astype(jnp.bfloat16)
    d_rows = (jnp.dot(d_hgate, fast_gate.T, preferred_element_type=jnp.float32) + jnp.dot(d_hup, fast_up.T, preferred_element_type=jnp.float32)).astype(jnp.bfloat16)
    grads = (jnp.dot(query_rows.T, d_hgate, preferred_element_type=jnp.float32), jnp.dot(query_rows.T, d_hup, preferred_element_type=jnp.float32), jnp.dot(active.T, grad_rows, preferred_element_type=jnp.float32))
    return (d_rows, grads)

def column_sums(matrices):
    return tuple((lax.optimization_barrier(jnp.sum(matrix * matrix, axis=0)) for matrix in matrices))

def apply_update(weight_rows, grad_parts, squares, full_width):
    scales = tuple((jnp.sqrt(square / full_width + EPSILON) for square in squares))
    fast_weights = tuple(((weight - STEP_SIZE * grad / scale).astype(jnp.bfloat16) for weight, grad, scale in zip(weight_rows, grad_parts, scales)))
    return (fast_weights, scales)

def back_products(query_parts, grad_parts):
    return tuple((lax.optimization_barrier(jnp.sum(-STEP_SIZE * dpart * gpart, axis=0)) for dpart, gpart in zip(query_parts, grad_parts)))

def normal_back(query_parts, grad_parts, scales, products, full_width):
    return tuple(((-STEP_SIZE * dpart / scale - gpart * product / (full_width * scale * scale * scale)).astype(jnp.bfloat16) for dpart, gpart, scale, product in zip(query_parts, grad_parts, scales, products)))

def reference(queries, key_tokens, values, out_grad, w_gate, w_up, w_down):
    weights = (w_gate, w_up, w_down)
    full_width = w_gate.shape[0]
    key_blocks = key_tokens.reshape(-1, TOK_DEV, full_width)
    value_blocks = values.reshape(-1, TOK_DEV, full_width)
    query_blocks = queries.reshape(-1, TOK_DEV, full_width)
    grad_blocks = out_grad.reshape(-1, TOK_DEV, full_width)
    zeros = tuple((jnp.zeros((full_width, full_width), jnp.float32) for weight in weights))

    def forward_step(summed, block):
        local = key_grad(w_gate, w_up, w_down, block[0], block[1])
        return (tuple((left + right for left, right in zip(summed, local))), None)
    grad_sum, unused = lax.scan(forward_step, zeros, (key_blocks, value_blocks))
    fast_weights, scales = apply_update(weights, grad_sum, column_sums(grad_sum), full_width)

    def query_step(summed, block):
        d_rows, local = query_grad(fast_weights, block[0], block[1])
        return (tuple((left + right for left, right in zip(summed, local))), d_rows)
    query_sum, d_query_blocks = lax.scan(query_step, zeros, (query_blocks, grad_blocks))
    rounded = normal_back(query_sum, grad_sum, scales, back_products(query_sum, grad_sum), full_width)
    rounded = lax.optimization_barrier(rounded)
    cotangent = tuple((item.astype(jnp.float32) for item in rounded))

    def second_step(summed, block):
        unused_out, pullback = jax.vjp(key_grad, w_gate, w_up, w_down, block[0], block[1])
        grads = pullback(cotangent)
        return (tuple((left + right for left, right in zip(summed, grads[:3]))), (grads[3], grads[4]))
    second_sum, pair = lax.scan(second_step, zeros, (key_blocks, value_blocks))
    inverse = 1.0 / TOKENS
    summed = tuple(((left + right) * inverse for left, right in zip(query_sum, second_sum)))
    return (d_query_blocks.reshape(-1, full_width), pair[0].reshape(-1, full_width), pair[1].reshape(-1, full_width), summed[0], summed[1], summed[2])
```

```python
import functools

import jax
import jax.numpy as jnp
from jax import lax
from jax.experimental import pallas as pl
from jax.experimental.pallas import tpu as pltpu
from jax.sharding import PartitionSpec as P

STEP_SIZE = 0.02
EPSILON = 1e-06
MESH = pl.DeviceIdType.MESH
BF = jnp.bfloat16
F32 = jnp.float32


def matmul(left, right):
    return jnp.dot(left.astype(BF), right.astype(BF), preferred_element_type=F32)


def key_grad(w_gate, w_up, w_down, key_rows, value_rows):
    hidden_gate = matmul(key_rows, w_gate)
    hidden_up = matmul(key_rows, w_up)
    sig = jax.nn.sigmoid(hidden_gate)
    active = hidden_gate * sig * hidden_up
    error = matmul(active, w_down) - value_rows
    d_active = matmul(error, w_down.T)
    d_hup = d_active * hidden_gate * sig
    d_hgate = d_active * hidden_up * sig * (1.0 + hidden_gate * (1.0 - sig))
    return (matmul(d_hgate.T, key_rows), matmul(d_hup.T, key_rows), matmul(error.T, active))


def query_grad(fast_t, query_rows, grad_rows):
    gate_t, up_t, down_t = fast_t
    hidden_gate = jnp.dot(query_rows, gate_t.T, preferred_element_type=F32)
    hidden_up = jnp.dot(query_rows, up_t.T, preferred_element_type=F32)
    sig = jax.nn.sigmoid(hidden_gate)
    active = (hidden_gate * sig * hidden_up).astype(BF)
    d_active = jnp.dot(grad_rows, down_t, preferred_element_type=F32)
    d_hup = (d_active * hidden_gate * sig).astype(BF)
    d_hgate = (d_active * hidden_up * sig * (1.0 + hidden_gate * (1.0 - sig))).astype(BF)
    d_rows = (
        jnp.dot(d_hgate, gate_t, preferred_element_type=F32)
        + jnp.dot(d_hup, up_t, preferred_element_type=F32)
    ).astype(BF)
    return (d_rows, active, d_hgate, d_hup)


def position(zs, gs):
    g = lax.axis_index("grp")
    t = lax.axis_index("tok")
    return g, t // 2, lax.rem(t, 2)


def greet(zs, gs, g, z, core):
    barrier = pltpu.get_barrier_semaphore()
    pl.semaphore_signal(barrier, inc=1, device_id=(g, 2 * z + 1 - core), device_id_type=MESH)
    for d in range(1, zs):
        peer = (g, 2 * lax.rem(z + d, zs) + core)
        pl.semaphore_signal(barrier, inc=1, device_id=peer, device_id_type=MESH)
    for d in range(1, gs):
        peer = (lax.rem(g + d, gs), 2 * z + core)
        pl.semaphore_signal(barrier, inc=1, device_id=peer, device_id_type=MESH)
    pl.semaphore_wait(barrier, zs + gs - 1)


def remote(src, dst, send, recv, peer):
    return pltpu.make_async_remote_copy(
        src_ref=src, dst_ref=dst, send_sem=send, recv_sem=recv,
        device_id=peer, device_id_type=MESH,
    )


def reduce_body(zs, gs, x, out, rc, s1, ra1, rb1, sa, sb, ra2, rb2,
                cs, cr, a1s, a1r, b1s, b1r, a2s, a2r, b2s, b2r):
    g, z, core = position(zs, gs)
    width = x.shape[-1]
    half = width // 2
    left, right = pl.ds(0, half), pl.ds(half, half)
    greet(zs, gs, g, z, core)
    twin = (g, 2 * z + 1 - core)
    pending = []
    pair = []
    order = list(range(1, zs)) + [0]
    for d in order:
        zc = lax.rem(z + d, zs)
        copy = remote(x.at[zc, 1 - core], rc.at[d], cs.at[d], cr.at[d], twin)
        copy.start()
        pair.append((d, zc, copy))
    first_a, first_b = [], []
    for d, zc, copy in pair:
        copy.wait_recv()
        for k in range(gs):
            s1[zc, k] = (x[zc, core, k].astype(F32) + rc[d, k].astype(F32)).astype(BF)
        if d:
            c = remote(s1.at[zc, :, :, left], ra1.at[d - 1], a1s.at[d - 1], a1r.at[d - 1],
                       (g, 2 * zc + core))
            c.start()
            first_a.append(c)
        for e in range(1, gs):
            gc = lax.rem(g + e, gs)
            c = remote(s1.at[zc, gc, :, right], rb1.at[e - 1, zc], b1s.at[e - 1, d],
                       b1r.at[e - 1, d], (gc, 2 * z + core))
            c.start()
            first_b.append((d, c))
    second = []
    for d in order:
        zc = lax.rem(z + d, zs)
        for dd, c in first_b:
            if dd == d:
                c.wait_recv()
        total = s1[zc, g, :, half:].astype(F32)
        for e in range(1, gs):
            total = total + rb1[e - 1, zc].astype(F32)
        if d:
            sb[d - 1] = total.astype(BF)
            c = remote(sb.at[d - 1], rb2.at[d - 1], b2s.at[d - 1], b2r.at[d - 1],
                       (g, 2 * zc + core))
            c.start()
            second.append(c)
        else:
            out[:, half:] = total
    for c in first_a:
        c.wait_recv()
    for e in list(range(1, gs)) + [0]:
        gc = lax.rem(g + e, gs)
        total = s1[z, gc, :, :half].astype(F32)
        for d in range(1, zs):
            total = total + ra1[d - 1, gc].astype(F32)
        if e:
            sa[e - 1] = total.astype(BF)
            c = remote(sa.at[e - 1], ra2.at[e - 1], a2s.at[e - 1], a2r.at[e - 1],
                       (gc, 2 * z + core))
            c.start()
            second.append(c)
        else:
            out[:, :half] = total
    for c in second:
        c.wait_recv()
    total = out[:, half:]
    for d in range(1, zs):
        total = total + rb2[d - 1].astype(F32)
    out[:, half:] = total
    total = out[:, :half]
    for e in range(1, gs):
        total = total + ra2[e - 1].astype(F32)
    out[:, :half] = total
    for d, zc, c in pair:
        c.wait_send()
    for c in first_a:
        c.wait_send()
    for d, c in first_b:
        c.wait_send()
    for c in second:
        c.wait_send()


VM = pltpu.VMEM
DMA = pltpu.SemaphoreType.DMA


def reduce_all(x, number):
    zs, _, gs, rows, width = x.shape
    half = width // 2
    return pl.pallas_call(
        functools.partial(reduce_body, zs, gs),
        out_shape=jax.ShapeDtypeStruct((rows, width), F32),
        in_specs=[pl.BlockSpec(memory_space=pltpu.VMEM)],
        out_specs=pl.BlockSpec(memory_space=pltpu.VMEM),
        scratch_shapes=[
            VM((zs, gs, rows, width), BF),
            VM((zs, gs, rows, width), BF),
            VM((zs - 1, gs, rows, half), BF),
            VM((gs - 1, zs, rows, half), BF),
            VM((gs - 1, rows, half), BF),
            VM((zs - 1, rows, half), BF),
            VM((gs - 1, rows, half), BF),
            VM((zs - 1, rows, half), BF),
            DMA((zs,)), DMA((zs,)),
            DMA((zs - 1,)), DMA((zs - 1,)),
            DMA((gs - 1, zs)), DMA((gs - 1, zs)),
            DMA((gs - 1,)), DMA((gs - 1,)),
            DMA((zs - 1,)), DMA((zs - 1,)),
        ],
        compiler_params=pltpu.CompilerParams(collective_id=number, has_side_effects=True),
    )(x)


def gather_body(zs, gs, y, out, cs, cr, a1s, a1r, b1s, b1r, a2s, a2r, b2s, b2r, ls):
    g, z, core = position(zs, gs)
    width = y.shape[-1]
    half = width // 2
    left, right = pl.ds(0, half), pl.ds(half, half)
    greet(zs, gs, g, z, core)
    twin = (g, 2 * z + 1 - core)
    own = pltpu.make_async_copy(y, out.at[z, core, g], ls)
    own.start()
    to_g = lambda e: (lax.rem(g + e, gs), 2 * z + core)
    to_z = lambda d: (g, 2 * lax.rem(z + d, zs) + core)
    first_a, first_b = [], []
    for e in range(1, gs):
        c = remote(y.at[:, left], out.at[z, core, g, :, left], a1s.at[e - 1], a1r.at[e - 1], to_g(e))
        c.start()
        first_a.append(c)
    for d in range(1, zs):
        c = remote(y.at[:, right], out.at[z, core, g, :, right], b1s.at[d - 1], b1r.at[d - 1], to_z(d))
        c.start()
        first_b.append(c)
    own.wait()
    sent = []
    second_a, second_b = [], []

    def hand(src, slot):
        c = remote(src, src, cs.at[slot], cr.at[slot], twin)
        c.start()
        sent.append(c)

    for c in first_a:
        c.wait_recv()
    for d in range(1, zs):
        part = out.at[z, core, :, :, left]
        c = remote(part, part, a2s.at[d - 1], a2r.at[d - 1], to_z(d))
        c.start()
        second_a.append(c)
    for c in first_b:
        c.wait_recv()
    for e in range(1, gs):
        part = out.at[:, core, g, :, right]
        c = remote(part, part, b2s.at[e - 1], b2r.at[e - 1], to_g(e))
        c.start()
        second_b.append(c)
    hand(out.at[z, core, :, :, left], 0)
    hand(out.at[:, core, g, :, right], 1)
    slot = 2
    for d in range(1, zs):
        second_a[d - 1].wait_recv()
        hand(out.at[lax.rem(z - d + zs, zs), core, :, :, left], slot)
        slot += 1
    for e in range(1, gs):
        second_b[e - 1].wait_recv()
        hand(out.at[:, core, lax.rem(g - e + gs, gs), :, right], slot)
        slot += 1
    for c in sent:
        c.wait()
    for c in first_a + first_b + second_a + second_b:
        c.wait_send()


def gather_all(y, zs, gs, number):
    rows, width = y.shape
    return pl.pallas_call(
        functools.partial(gather_body, zs, gs),
        out_shape=jax.ShapeDtypeStruct((zs, 2, gs, rows, width), BF),
        in_specs=[pl.BlockSpec(memory_space=pltpu.VMEM)],
        out_specs=pl.BlockSpec(memory_space=pltpu.VMEM),
        scratch_shapes=[
            DMA((zs + gs,)), DMA((zs + gs,)),
            DMA((gs - 1,)), DMA((gs - 1,)),
            DMA((zs - 1,)), DMA((zs - 1,)),
            DMA((zs - 1,)), DMA((zs - 1,)),
            DMA((gs - 1,)), DMA((gs - 1,)),
            DMA,
        ],
        compiler_params=pltpu.CompilerParams(collective_id=number, has_side_effects=True),
    )(y)


def on_device(queries, key_tokens, values, out_grad, w_gate, w_up, w_down):
    gs, toks = lax.axis_size("grp"), lax.axis_size("tok")
    zs, devices = toks // 2, gs * toks
    full_width = w_gate.shape[0]
    tokens_all = key_tokens.shape[0] * devices
    weights = (w_gate, w_up, w_down)
    rows = 3 * full_width // devices
    direct = 3 * full_width % (8 * devices) == 0 and toks % 4 == 0 and full_width % 256 == 0
    me = lax.axis_index("tok") * gs + lax.axis_index("grp")

    def reduce_units(x, number):
        if direct:
            return reduce_all(x.astype(BF).reshape(zs, 2, gs, rows, full_width), number)
        y = x.reshape(toks, gs * rows, full_width)
        y = lax.psum_scatter(y, "tok", scatter_dimension=0, tiled=True)[0]
        return lax.psum_scatter(y.reshape(gs, rows, full_width), "grp", scatter_dimension=0, tiled=True)[0]

    def gather_units(y, number):
        if direct:
            full = gather_all(y, zs, gs, number)
        else:
            full = lax.all_gather(lax.all_gather(y, "grp"), "tok")
        full = full.reshape(3, full_width, full_width)
        return full[0], full[1], full[2]

    local_grad, pullback = jax.vjp(key_grad, w_gate, w_up, w_down, key_tokens, values)
    grad = reduce_units(jnp.stack(local_grad), 0)
    scale = jnp.sqrt(jnp.sum(grad * grad, axis=1, keepdims=True) / full_width + EPSILON)
    mine = lax.dynamic_slice_in_dim(jnp.concatenate(weights, axis=1), me * rows, rows, 1).T
    fast = (mine - STEP_SIZE * grad / scale).astype(BF)
    fast_t = gather_units(fast, 1)
    d_queries, active, d_hgate, d_hup = query_grad(fast_t, queries, out_grad)
    dot = functools.partial(jnp.dot, preferred_element_type=F32)
    query_local = jnp.stack((dot(d_hgate.T, queries), dot(d_hup.T, queries), dot(out_grad.T, active)))
    query_part = reduce_units(query_local, 2)
    product = jnp.sum(-STEP_SIZE * query_part * grad, axis=1, keepdims=True)
    cot = (
        -STEP_SIZE * query_part / scale - grad * product / (full_width * scale * scale * scale)
    ).astype(BF)
    cotangent = tuple(item.astype(F32) for item in gather_units(cot, 3))
    second = pullback(cotangent)
    plain = (dot(queries.T, d_hgate), dot(queries.T, d_hup), dot(active.T, out_grad))
    combined = jnp.stack(tuple((left + right for left, right in zip(plain, second[:3]))))
    combined = combined.reshape(3, toks, full_width // toks, full_width).transpose(1, 0, 2, 3)
    summed = reduce_units(combined, 4) * (1.0 / tokens_all)
    summed = lax.all_gather(summed.astype(BF), "grp").astype(F32)
    summed = summed.reshape(3, full_width // toks, full_width)
    return (d_queries, second[3], second[4], summed[0], summed[1], summed[2])


def solution(mesh):
    token = P(("grp", "tok"), None)
    return jax.shard_map(
        on_device,
        mesh=mesh,
        in_specs=(token, token, token, token, P(), P(), P()),
        out_specs=(token, token, token, P("tok", None), P("tok", None), P("tok", None)),
        check_vma=False,
    )
```

```python
import functools

import jax
import jax.numpy as jnp
from jax import lax
from jax.experimental import pallas as pl
from jax.experimental.pallas import tpu as pltpu
from jax.sharding import PartitionSpec as P

STEP_SIZE = 0.02
EPSILON = 1e-06
MESH = pl.DeviceIdType.MESH
BF = jnp.bfloat16
F32 = jnp.float32


def matmul(left, right):
    return jnp.dot(left.astype(BF), right.astype(BF), preferred_element_type=F32)


def key_grad(w_gate, w_up, w_down, key_rows, value_rows):
    hidden_gate = matmul(key_rows, w_gate)
    hidden_up = matmul(key_rows, w_up)
    sig = jax.nn.sigmoid(hidden_gate)
    active = hidden_gate * sig * hidden_up
    error = matmul(active, w_down) - value_rows
    d_active = matmul(error, w_down.T)
    d_hup = d_active * hidden_gate * sig
    d_hgate = d_active * hidden_up * sig * (1.0 + hidden_gate * (1.0 - sig))
    return (matmul(d_hgate.T, key_rows), matmul(d_hup.T, key_rows), matmul(error.T, active))


def query_grad(fast_t, query_rows, grad_rows):
    gate_t, up_t, down_t = fast_t
    hidden_gate = jnp.dot(query_rows, gate_t.T, preferred_element_type=F32)
    hidden_up = jnp.dot(query_rows, up_t.T, preferred_element_type=F32)
    sig = jax.nn.sigmoid(hidden_gate)
    active = (hidden_gate * sig * hidden_up).astype(BF)
    d_active = jnp.dot(grad_rows, down_t, preferred_element_type=F32)
    d_hup = (d_active * hidden_gate * sig).astype(BF)
    d_hgate = (d_active * hidden_up * sig * (1.0 + hidden_gate * (1.0 - sig))).astype(BF)
    d_rows = (
        jnp.dot(d_hgate, gate_t, preferred_element_type=F32)
        + jnp.dot(d_hup, up_t, preferred_element_type=F32)
    ).astype(BF)
    return (d_rows, active, d_hgate, d_hup)


def cut_of(width):
    return 128 * (width // 384)


def position(zs, gs):
    g = lax.axis_index("grp")
    t = lax.axis_index("tok")
    return g, t // 2, lax.rem(t, 2)


def greet(zs, gs, g, z, core):
    barrier = pltpu.get_barrier_semaphore()
    pl.semaphore_signal(barrier, inc=1, device_id=(g, 2 * z + 1 - core), device_id_type=MESH)
    for d in range(1, zs):
        peer = (g, 2 * lax.rem(z + d, zs) + core)
        pl.semaphore_signal(barrier, inc=1, device_id=peer, device_id_type=MESH)
    for d in range(1, gs):
        peer = (lax.rem(g + d, gs), 2 * z + core)
        pl.semaphore_signal(barrier, inc=1, device_id=peer, device_id_type=MESH)
    pl.semaphore_wait(barrier, zs + gs - 1)


def remote(src, dst, send, recv, peer):
    return pltpu.make_async_remote_copy(
        src_ref=src, dst_ref=dst, send_sem=send, recv_sem=recv,
        device_id=peer, device_id_type=MESH,
    )


def reduce_body(zs, gs, x, out, rc, s1, ra1, rb1, sa, sb, ra2, rb2,
                cs, cr, a1s, a1r, b1s, b1r, a2s, a2r, b2s, b2r):
    g, z, core = position(zs, gs)
    width = x.shape[-1]
    half = cut_of(width)
    left, right = pl.ds(0, half), pl.ds(half, width - half)
    greet(zs, gs, g, z, core)
    twin = (g, 2 * z + 1 - core)
    pending = []
    pair = []
    order = list(range(1, zs)) + [0]
    for d in order:
        zc = lax.rem(z + d, zs)
        copy = remote(x.at[zc, 1 - core], rc.at[d], cs.at[d], cr.at[d], twin)
        copy.start()
        pair.append((d, zc, copy))
    first_a, first_b = [], []
    for d, zc, copy in pair:
        copy.wait_recv()
        for k in range(gs):
            s1[zc, k] = (x[zc, core, k].astype(F32) + rc[d, k].astype(F32)).astype(BF)
        if d:
            c = remote(s1.at[zc, :, :, left], ra1.at[d - 1], a1s.at[d - 1], a1r.at[d - 1],
                       (g, 2 * zc + core))
            c.start()
            first_a.append(c)
        for e in range(1, gs):
            gc = lax.rem(g + e, gs)
            c = remote(s1.at[zc, gc, :, right], rb1.at[e - 1, zc], b1s.at[e - 1, d],
                       b1r.at[e - 1, d], (gc, 2 * z + core))
            c.start()
            first_b.append((d, c))
    second = []
    for d in order:
        zc = lax.rem(z + d, zs)
        for dd, c in first_b:
            if dd == d:
                c.wait_recv()
        total = s1[zc, g, :, half:].astype(F32)
        for e in range(1, gs):
            total = total + rb1[e - 1, zc].astype(F32)
        if d:
            sb[d - 1] = total.astype(BF)
            c = remote(sb.at[d - 1], rb2.at[d - 1], b2s.at[d - 1], b2r.at[d - 1],
                       (g, 2 * zc + core))
            c.start()
            second.append(c)
        else:
            out[:, half:] = total
    for c in first_a:
        c.wait_recv()
    for e in list(range(1, gs)) + [0]:
        gc = lax.rem(g + e, gs)
        total = s1[z, gc, :, :half].astype(F32)
        for d in range(1, zs):
            total = total + ra1[d - 1, gc].astype(F32)
        if e:
            sa[e - 1] = total.astype(BF)
            c = remote(sa.at[e - 1], ra2.at[e - 1], a2s.at[e - 1], a2r.at[e - 1],
                       (gc, 2 * z + core))
            c.start()
            second.append(c)
        else:
            out[:, :half] = total
    for c in second:
        c.wait_recv()
    total = out[:, half:]
    for d in range(1, zs):
        total = total + rb2[d - 1].astype(F32)
    out[:, half:] = total
    total = out[:, :half]
    for e in range(1, gs):
        total = total + ra2[e - 1].astype(F32)
    out[:, :half] = total
    for d, zc, c in pair:
        c.wait_send()
    for c in first_a:
        c.wait_send()
    for d, c in first_b:
        c.wait_send()
    for c in second:
        c.wait_send()


VM = pltpu.VMEM
DMA = pltpu.SemaphoreType.DMA


def reduce_gather_body(zs, gs, x, full, part, fs, fr, *scratch):
    reduce_body(zs, gs, x, part, *scratch)
    g, z, core = position(zs, gs)
    full[g] = part[...].astype(BF)
    copies = []
    for e in range(1, gs):
        peer = (lax.rem(g + e, gs), 2 * z + core)
        c = remote(full.at[g], full.at[g], fs.at[e - 1], fr.at[e - 1], peer)
        c.start()
        copies.append(c)
    for c in copies:
        c.wait()


def reduce_all(x, number, gathered=False):
    zs, _, gs, rows, width = x.shape
    left = cut_of(width)
    right = width - left
    scratch = [
        VM((zs, gs, rows, width), BF),
        VM((zs, gs, rows, width), BF),
        VM((zs - 1, gs, rows, left), BF),
        VM((gs - 1, zs, rows, right), BF),
        VM((gs - 1, rows, left), BF),
        VM((zs - 1, rows, right), BF),
        VM((gs - 1, rows, left), BF),
        VM((zs - 1, rows, right), BF),
        DMA((zs,)), DMA((zs,)),
        DMA((zs - 1,)), DMA((zs - 1,)),
        DMA((gs - 1, zs)), DMA((gs - 1, zs)),
        DMA((gs - 1,)), DMA((gs - 1,)),
        DMA((zs - 1,)), DMA((zs - 1,)),
    ]
    shape = jax.ShapeDtypeStruct((rows, width), F32)
    body = reduce_body
    if gathered:
        shape = jax.ShapeDtypeStruct((gs, rows, width), BF)
        body = reduce_gather_body
        scratch = [VM((rows, width), F32), DMA((gs - 1,)), DMA((gs - 1,))] + scratch
    return pl.pallas_call(
        functools.partial(body, zs, gs),
        out_shape=shape,
        in_specs=[pl.BlockSpec(memory_space=pltpu.VMEM)],
        out_specs=pl.BlockSpec(memory_space=pltpu.VMEM),
        scratch_shapes=scratch,
        compiler_params=pltpu.CompilerParams(collective_id=number, has_side_effects=True),
    )(x)


def gather_body(zs, gs, y, out, cs, cr, a1s, a1r, b1s, b1r, a2s, a2r, b2s, b2r, ls):
    g, z, core = position(zs, gs)
    width = y.shape[-1]
    half = cut_of(width)
    left, right = pl.ds(0, half), pl.ds(half, width - half)
    greet(zs, gs, g, z, core)
    twin = (g, 2 * z + 1 - core)
    own = pltpu.make_async_copy(y, out.at[z, core, g], ls)
    own.start()
    to_g = lambda e: (lax.rem(g + e, gs), 2 * z + core)
    to_z = lambda d: (g, 2 * lax.rem(z + d, zs) + core)
    first_a, first_b = [], []
    for e in range(1, gs):
        c = remote(y.at[:, left], out.at[z, core, g, :, left], a1s.at[e - 1], a1r.at[e - 1], to_g(e))
        c.start()
        first_a.append(c)
    for d in range(1, zs):
        c = remote(y.at[:, right], out.at[z, core, g, :, right], b1s.at[d - 1], b1r.at[d - 1], to_z(d))
        c.start()
        first_b.append(c)
    own.wait()
    sent = []
    second_a, second_b = [], []

    def hand(src, slot):
        c = remote(src, src, cs.at[slot], cr.at[slot], twin)
        c.start()
        sent.append(c)

    for c in first_a:
        c.wait_recv()
    for d in range(1, zs):
        part = out.at[z, core, :, :, left]
        c = remote(part, part, a2s.at[d - 1], a2r.at[d - 1], to_z(d))
        c.start()
        second_a.append(c)
    for c in first_b:
        c.wait_recv()
    for e in range(1, gs):
        part = out.at[:, core, g, :, right]
        c = remote(part, part, b2s.at[e - 1], b2r.at[e - 1], to_g(e))
        c.start()
        second_b.append(c)
    hand(out.at[z, core, :, :, left], 0)
    hand(out.at[:, core, g, :, right], 1)
    slot = 2
    for d in range(1, zs):
        second_a[d - 1].wait_recv()
        hand(out.at[lax.rem(z - d + zs, zs), core, :, :, left], slot)
        slot += 1
    for e in range(1, gs):
        second_b[e - 1].wait_recv()
        hand(out.at[:, core, lax.rem(g - e + gs, gs), :, right], slot)
        slot += 1
    for c in sent:
        c.wait()
    for c in first_a + first_b + second_a + second_b:
        c.wait_send()


def gather_all(y, zs, gs, number):
    rows, width = y.shape
    return pl.pallas_call(
        functools.partial(gather_body, zs, gs),
        out_shape=jax.ShapeDtypeStruct((zs, 2, gs, rows, width), BF),
        in_specs=[pl.BlockSpec(memory_space=pltpu.VMEM)],
        out_specs=pl.BlockSpec(memory_space=pltpu.VMEM),
        scratch_shapes=[
            DMA((zs + gs,)), DMA((zs + gs,)),
            DMA((gs - 1,)), DMA((gs - 1,)),
            DMA((zs - 1,)), DMA((zs - 1,)),
            DMA((zs - 1,)), DMA((zs - 1,)),
            DMA((gs - 1,)), DMA((gs - 1,)),
            DMA,
        ],
        compiler_params=pltpu.CompilerParams(collective_id=number, has_side_effects=True),
    )(y)


def on_device(queries, key_tokens, values, out_grad, w_gate, w_up, w_down):
    gs, toks = lax.axis_size("grp"), lax.axis_size("tok")
    zs, devices = toks // 2, gs * toks
    full_width = w_gate.shape[0]
    tokens_all = key_tokens.shape[0] * devices
    weights = (w_gate, w_up, w_down)
    rows = 3 * full_width // devices
    direct = 3 * full_width % (8 * devices) == 0 and toks % 4 == 0 and full_width % 384 == 0
    me = lax.axis_index("tok") * gs + lax.axis_index("grp")

    def reduce_units(x, number):
        if direct:
            return reduce_all(x.astype(BF).reshape(zs, 2, gs, rows, full_width), number)
        y = x.reshape(toks, gs * rows, full_width)
        y = lax.psum_scatter(y, "tok", scatter_dimension=0, tiled=True)[0]
        return lax.psum_scatter(y.reshape(gs, rows, full_width), "grp", scatter_dimension=0, tiled=True)[0]

    def gather_units(y, number):
        if direct:
            full = gather_all(y, zs, gs, number)
        else:
            full = lax.all_gather(lax.all_gather(y, "grp"), "tok")
        full = full.reshape(3, full_width, full_width)
        return full[0], full[1], full[2]

    local_grad, pullback = jax.vjp(key_grad, w_gate, w_up, w_down, key_tokens, values)
    grad = reduce_units(jnp.stack(local_grad), 0)
    scale = jnp.sqrt(jnp.sum(grad * grad, axis=1, keepdims=True) / full_width + EPSILON)
    mine = lax.dynamic_slice_in_dim(jnp.concatenate(weights, axis=1), me * rows, rows, 1).T
    fast = (mine - STEP_SIZE * grad / scale).astype(BF)
    fast_t = gather_units(fast, 1)
    d_queries, active, d_hgate, d_hup = query_grad(fast_t, queries, out_grad)
    dot = functools.partial(jnp.dot, preferred_element_type=F32)
    query_local = jnp.stack((dot(d_hgate.T, queries), dot(d_hup.T, queries), dot(out_grad.T, active)))
    query_part = reduce_units(query_local, 2)
    product = jnp.sum(-STEP_SIZE * query_part * grad, axis=1, keepdims=True)
    cot = (
        -STEP_SIZE * query_part / scale - grad * product / (full_width * scale * scale * scale)
    ).astype(BF)
    cotangent = tuple(item.astype(F32) for item in gather_units(cot, 3))
    second = pullback(cotangent)
    plain = (dot(queries.T, d_hgate), dot(queries.T, d_hup), dot(active.T, out_grad))
    combined = jnp.stack(tuple((left + right for left, right in zip(plain, second[:3]))))
    combined = combined.reshape(3, toks, full_width // toks, full_width).transpose(1, 0, 2, 3)
    if direct:
        units = combined.astype(BF).reshape(zs, 2, gs, rows, full_width)
        summed = reduce_all(units, 4, True)
    else:
        summed = lax.all_gather(reduce_units(combined, 4).astype(BF), "grp")
    summed = summed.astype(F32) * (1.0 / tokens_all)
    summed = summed.reshape(3, full_width // toks, full_width)
    return (d_queries, second[3], second[4], summed[0], summed[1], summed[2])


def solution(mesh):
    token = P(("grp", "tok"), None)
    return jax.shard_map(
        on_device,
        mesh=mesh,
        in_specs=(token, token, token, token, P(), P(), P()),
        out_specs=(token, token, token, P("tok", None), P("tok", None), P("tok", None)),
        check_vma=False,
    )
```
